32 devices in a mesh: row: 8 (over z, y), col: 4 (over x, core).
Axes of the slice: x: 2, y: 2, z: 4, core: 2. Of those that a mesh axis runs over, the one named last changes fastest.
Arguments:
- env: float32 [512, 32768], P('row', 'col'), may hold values from -0.03125 to 0.03125
- wave: float32 [32768, 512], P('row', 'col'), may hold values from -6 to 6
- mpo: float32 [16, 16], replicated, may hold values from -1.5 to 1.5
Outputs:
- applied: float32 [512, 512], P('row', 'col')
The draws below stay inside these ranges and needn't reach their ends.
All inputs are finite; a program needn't handle non-finite values.
Results may differ from the reference program's by a relative error of at most 0.00007.
Values sent between devices are 32-bit elements; how exact they have to be, the bound alone decides.
No kernel may reach another device: no remote copies, remote signals or barrier semaphores. Data moves between devices by JAX's collectives and lax.ppermute only.
A program may use at most 128 MiB of HBM per device.

```python
import jax
import jax.numpy as jnp
from jax import lax

L = 32768
S = 16
ROWS = 512
R = 32


def levels(stream_key, shape, shards, least, high):
    loudness = 1.0
    for position, blocks in shards:
        heights = jax.random.uniform(jax.random.fold_in(jax.random.fold_in(stream_key, 6), position), (blocks,), jnp.float32, least / len(shards), high / len(shards))
        loudness = loudness * jnp.repeat(jnp.exp(heights), shape[position] // blocks).reshape((-1,) + (1,) * (len(shape) - 1 - position))
    return loudness


def gaussian(rng, shape, scale, most, pieces=(), kind=jnp.bfloat16):
    factor_of = levels(rng, shape, pieces, -0.22, 0.18) if pieces else 1.0
    values = jax.random.normal(rng, shape, jnp.float32) * scale * factor_of
    return jnp.minimum(jnp.maximum(values, -most), most).astype(kind)


def setup_inputs(seed: int = 0) -> dict:
    key_of = jax.random.split(jax.random.key(seed), 4)
    env = gaussian(key_of[0], (ROWS, L), L ** -0.5, 0.03125, ((0, 8), (1, 4)), jnp.float32)
    wave = gaussian(key_of[1], (L, R * S), 1.0, 6.0, ((0, 8), (1, 4)), jnp.float32)
    mpo = gaussian(key_of[2], (S, S), S ** -0.5, 1.5, (), jnp.float32)
    return dict(env=env, wave=wave, mpo=mpo)


def reference(env, wave, mpo):
    spins = mpo.shape[0]
    left = wave.shape[0]
    right = wave.shape[1] // spins
    wave3 = wave.reshape(left, right, spins)
    mixed = jnp.einsum("krs,st->ktr", wave3, mpo, precision=lax.Precision.HIGHEST)
    flat = mixed.reshape(left, spins * right)
    return jnp.dot(env, flat, precision=lax.Precision.HIGHEST, preferred_element_type=jnp.float32)
```

```python
import jax
import jax.numpy as jnp
from jax import lax
from jax.sharding import PartitionSpec as P

AXES = ("row", "col")
CHUNKS = 2


def pick(parts, index):
    if len(parts) == 1:
        return parts[0]
    if len(parts) == 2:
        return jnp.where(index == 0, parts[0], parts[1])
    return lax.dynamic_index_in_dim(jnp.stack(parts), index, 0, keepdims=False)


def make_shards(rows_n, cols_n):
    planes = cols_n
    Y = rows_n // planes
    X = cols_n // 2

    def shards(env, wave, mpo):
        row = lax.axis_index("row")
        col = lax.axis_index("col")
        z, y = row // Y, row % Y
        x, core = col // 2, col % 2
        spins = mpo.shape[0]
        width = wave.shape[1]
        cols = width * cols_n
        right = cols // spins
        deep = env.shape[1] // (Y * X)
        out_w = cols // cols_n

        def move(value, to):
            pairs = []
            for zz in range(planes):
                for yy in range(Y):
                    for xx in range(X):
                        for kk in range(2):
                            a, b, c, d = to(zz, yy, xx, kk)
                            pairs.append(((zz * Y + yy) * cols_n + xx * 2 + kk, (a * Y + b) * cols_n + c * 2 + d))
            return lax.ppermute(value, AXES, pairs)

        have = []
        for dx in range(X):
            part = lax.dynamic_slice(wave, ((x ^ dx) * deep, 0), (deep, width))
            have.append(part if dx == 0 else move(part, lambda a, b, c, d: (a, b, c ^ dx, d)))
        mine = jnp.concatenate(have, axis=1)
        other = move(mine, lambda a, b, c, d: (a, b, c, d ^ 1))

        def mixing(which):
            i = jnp.arange(X * width)[:, None]
            j = jnp.arange(cols)[None, :]
            spin_in = (i % spins == jnp.arange(spins)[None, :]).astype(jnp.float32)
            spin_out = (jnp.arange(spins)[:, None] == j // right).astype(jnp.float32)
            full = jnp.dot(jnp.dot(spin_in, mpo, precision=lax.Precision.HIGHEST), spin_out, precision=lax.Precision.HIGHEST)
            owner = (x ^ (i // width)) * 2 + which
            r = owner * (width // spins) + (i % width) // spins
            return jnp.where(r == j % right, full, 0.0)

        mixed = jnp.dot(mine, mixing(core), precision=lax.Precision.HIGH, preferred_element_type=jnp.float32) + jnp.dot(
            other, mixing(core ^ 1), precision=lax.Precision.HIGH, preferred_element_type=jnp.float32
        )

        def gather(first, count):
            got = []
            for dx in range(X):
                line = []
                for dy in range(Y):
                    part = lax.dynamic_slice(env, (first, ((y ^ dy) * X + (x ^ dx)) * deep), (count, deep))
                    line.append(part if dx == 0 and dy == 0 else move(part, lambda a, b, c, d: (a, b ^ dy, c ^ dx, d)))
                got.append(jnp.concatenate(line, axis=0))
            return got

        def cross(got):
            out = [None] * X
            for b in reversed(range(X)):
                out[b] = move(pick(got, x ^ b ^ (z >> 1)), lambda a, bb, c, d: (2 * (b ^ (a >> 1)) + d, bb, c, a & 1))
            return jnp.concatenate(out, axis=0)

        def scatter(part, count):
            part = part.reshape(X * Y * count, X, 2 * out_w)
            keep = None
            pieces = [lax.dynamic_index_in_dim(part, x ^ dx, 1, keepdims=False) for dx in range(X)]
            keep = pieces[0]
            for dx in range(1, X):
                keep = keep + move(pieces[dx], lambda a, b, c, d: (a, b, c ^ dx, d))
            keep = keep.reshape(X, Y, count, 2 * out_w)
            total = keep[:, 0]
            for dy in range(1, Y):
                total = total + move(keep[:, dy], lambda a, b, c, d: (a, b ^ dy, c, d))
            low, high = total[..., :out_w], total[..., out_w:]
            stay = pick([low, high], core)
            away = move(pick([high, low], core), lambda a, b, c, d: (a, b, c, d ^ 1))
            both = jnp.stack([stay, away])
            acc = both[:, 0]
            for b in range(1, X):
                acc = acc + move(both[:, b], lambda a, bb, c, d: (2 * ((a >> 1) ^ b) + (a & 1), bb, c, d))
            side = core ^ (z & 1)
            return pick([acc[0], acc[1]], side) + move(pick([acc[1], acc[0]], side), lambda a, b, c, d: (a ^ 1, b, c, d))

        count = env.shape[0] // CHUNKS
        outs = []
        for q in range(CHUNKS):
            block = cross(gather(q * count, count))
            part = jnp.dot(block, mixed, precision=lax.Precision.HIGH, preferred_element_type=jnp.float32)
            outs.append(scatter(part, count))
        return jnp.concatenate(outs, axis=0)

    return shards


def solution(mesh):
    shards = make_shards(mesh.shape["row"], mesh.shape["col"])
    in_specs = (P("row", "col"), P("row", "col"), P())
    return jax.shard_map(shards, mesh=mesh, in_specs=in_specs, out_specs=P("row", "col"), check_vma=False)
```
